1024 devices in a mesh: segment: 8 (over y), expert: 64 (over z, x), dp: 2 (over core).
Axes of the slice: x: 8, y: 8, z: 8, core: 2. Of those that a mesh axis runs over, the one named last changes fastest.
Arguments:
- activations: bfloat16 [8, 4096, 8, 512], P('segment', ('expert', 'dp')), may hold values from -6 to 6
- upstream: bfloat16 [8, 4096, 8, 512], P('segment', ('expert', 'dp')), may hold values from -6 to 6
- routes: int32 [8, 4096, 2], P('segment', ('expert', 'dp')), may hold values from 0 to 63, all different within a row; in each aligned block of 32 rows (0 to 31, 32 to 63, ..., all dimensions but the last counted through in order) at most 2 rows name the same one
- gate_codes: int32 [8, 4096, 2], P('segment', ('expert', 'dp')), may hold values from 1 to 32767
- weights: bfloat16 [8, 64, 9, 64, 512], P('segment', 'expert'), may hold values from -0.25 to 0.25
Outputs:
- input_grad: bfloat16 [8, 4096, 8, 512], P('segment', ('expert', 'dp'))
- weight_grad: float32 [8, 64, 9, 64, 512], P('segment', 'expert')
The draws below stay inside these ranges and needn't reach their ends.
Inputs may be any that keep to these rules, and one draw needn't show every extreme that they name: `routes`: the two experts of a tile differ; the 32 tiles of one device name each expert at most 2 times, and on some devices one expert exactly 2 times.
All inputs are finite; a program needn't handle non-finite values.
Results may differ from the reference program's by a relative error of at most 0.004.
Values may be sent and summed in bfloat16 or wider, within the bound.
A program may use at most 64 MiB of HBM per device.

```python
import math
import jax
import jax.numpy as jnp
import numpy as np
from jax import lax

C = 512
GW = 64
TH = 4
TW = 2
CELLS = 8
TPD = 32
EXPERTS = 64
CAP = 2
SEGMENTS = 8
TILES = 4096
N_EXPERT = 64
N_DP = 2


def touch_ends(array, own_key, smallest, top_value):
    longest = array.shape.index(max(array.shape))
    spots = []
    for shift in (0, 1):
        where = [jax.random.randint(jax.random.fold_in(own_key, axis), (), 0, length) for axis, length in enumerate(array.shape)]
        where[longest] = (where[longest] + shift) % array.shape[longest]
        spots.append(tuple(where))
    return array.at[spots[0]].set(smallest).at[spots[1]].set(top_value)


def level_of(key, dims, split, least, top_value):
    level = 1.0
    for axis_at, parts in split:
        draws = jax.random.uniform(jax.random.fold_in(jax.random.fold_in(key, 6), axis_at), (parts,), jnp.float32, least / len(split), top_value / len(split))
        level = level * jnp.repeat(jnp.exp(draws), dims[axis_at] // parts).reshape((-1,) + (1,) * (len(dims) - 1 - axis_at))
    return level


def deal_out(rng, own, number, rows, amount, top, reach, slope):
    order = jax.random.permutation(rng, amount)
    packed, ordinary = portions_of(amount, rows * top, reach, slope, True), portions_of(amount, rows * top, reach, slope, False)
    places = jnp.arange(amount)

    def named(lengths, rotation):
        used = int((lengths > 0).sum())
        fixed = max(1, used // 4)
        passed = fixed + (places - fixed + rotation * (used - fixed)) % max(1, amount - fixed)
        return jnp.zeros((amount,), jnp.int32).at[order[jnp.where(places < fixed, places, passed)]].set(jnp.asarray(lengths, jnp.int32))

    lengths = jnp.where(number % 4 == 0, named(packed, number // 4), named(ordinary, number - number // 4 - 1))
    mixed = jax.random.permutation(jax.random.fold_in(own, 3), amount)
    giver, receiver = mixed[0:amount // 2 * 2:2], mixed[1:amount // 2 * 2:2]
    room = jnp.minimum(lengths[giver] - 1, reach - lengths[receiver]) // 2
    room = jnp.where((giver == order[0]) | (receiver == order[0]) | (lengths[receiver] == 0), 0, jnp.maximum(room, 0))
    passed = jax.random.randint(jax.random.fold_in(own, 4), (amount // 2,), 0, 1 << 20) % (room + 1)
    lengths = lengths.at[giver].add(-passed).at[receiver].add(passed)
    items = jnp.searchsorted(jnp.cumsum(lengths), jnp.arange(rows * top), side="right").astype(jnp.int32)
    listing = items.reshape(top, rows).T
    listing = listing[jax.random.permutation(jax.random.fold_in(own, 1), rows)]
    rotation = jax.random.randint(jax.random.fold_in(own, 2), (rows, 1), 0, top)
    return jnp.take_along_axis(listing, (jnp.arange(top)[None, :] + rotation) % top, axis=1)


def portions_of(count, total, limit, lean, full):
    loads = [(1 << 20) // math.isqrt(rank ** lean) + 1 for rank in range(1, count + 1)]
    largest = limit if full else min(limit, max(-(-total // count), total * loads[0] // sum(loads)))
    least = 1 if total - largest >= count - 1 else 0
    counts, surplus = [largest] + [least] * (count - 1), total - largest - least * (count - 1)
    while surplus > 0:
        candidates = [i for i in range(1, count) if counts[i] < largest] or [i for i in range(1, count) if counts[i] < limit]
        pool, budget = sum([loads[i] for i in candidates]), surplus
        for i in candidates:
            extra = min(limit - counts[i], max(1, budget * loads[i] // pool), surplus)
            counts[i] = counts[i] + extra
            surplus = surplus - extra
    return np.array(counts)


def centred(rng, shape, width, bound, shards=(), kind=jnp.bfloat16):
    entries = width * jax.random.normal(rng, shape, jnp.float32)
    if shards:
        entries = entries * level_of(rng, shape, shards, -0.22, 0.18)
    return jnp.clip(entries, -bound, bound).astype(kind)


def setup_inputs(seed: int = 0) -> dict:
    splits = jax.random.split(jax.random.key(seed), 6)
    activations = centred(splits[0], (SEGMENTS, TILES, CELLS, C), 1.0, 6.0, ((0, 8), (1, 128)))
    upstream = centred(splits[1], (SEGMENTS, TILES, CELLS, C), 1.0, 6.0, ((0, 8), (1, 128)))
    routes_keys = jax.random.split(jax.random.fold_in(splits[2], 1), SEGMENTS * TILES // TPD)
    routes_turns = jax.random.permutation(jax.random.fold_in(splits[2], 3), SEGMENTS * TILES // TPD)
    routes = jax.vmap(lambda own, number: deal_out(jax.random.fold_in(splits[2], 2), own, number, TPD, EXPERTS, 2, CAP, 2))(routes_keys, routes_turns).reshape((SEGMENTS, TILES, 2))
    gate_codes = touch_ends(jax.random.randint(splits[3], (SEGMENTS, TILES, 2), 1, 32768), jax.random.fold_in(splits[3], 1), 1, 32767).astype(jnp.int32)
    weights = centred(splits[4], (SEGMENTS, EXPERTS, 9, GW, C), (9 * GW) ** -0.5, 0.25, ((0, 8), (1, 64)))
    return {"activations": activations, "upstream": upstream, "routes": routes, "gate_codes": gate_codes, "weights": weights}


def transpose_conv(scaled_grads, weight):
    tile_count = scaled_grads.shape[0]
    group_width = weight.shape[1]
    channels = weight.shape[2]
    group_count = channels // group_width
    padded = jnp.pad(scaled_grads.reshape(tile_count, TH, TW, channels), ((0, 0), (1, 1), (1, 1), (0, 0)))
    summed = jnp.zeros((tile_count, TH, TW, group_count, group_width), jnp.float32)
    for row_off in (-1, 0, 1):
        for col_off in (-1, 0, 1):
            tap_index = (row_off + 1) * 3 + (col_off + 1)
            shifted = padded[:, 1 - row_off:1 - row_off + TH, 1 - col_off:1 - col_off + TW, :]
            shifted = shifted.reshape(tile_count, TH, TW, group_count, group_width).astype(jnp.float32)
            kernel = weight[tap_index].reshape(group_width, group_count, group_width).astype(jnp.float32)
            summed = summed + jnp.einsum('nijgo,cgo->nijgc', shifted, kernel)
    return summed.reshape(tile_count, TH * TW, channels)


def weight_corr(inputs, scaled_grads, group_width):
    tile_count = inputs.shape[0]
    channels = inputs.shape[2]
    group_count = channels // group_width
    padded = jnp.pad(inputs.reshape(tile_count, TH, TW, channels), ((0, 0), (1, 1), (1, 1), (0, 0)))
    grads = scaled_grads.reshape(tile_count, TH, TW, group_count, group_width).astype(jnp.float32)
    taps = []
    for row_off in (-1, 0, 1):
        for col_off in (-1, 0, 1):
            shifted = padded[:, 1 + row_off:1 + row_off + TH, 1 + col_off:1 + col_off + TW, :]
            shifted = shifted.reshape(tile_count, TH, TW, group_count, group_width).astype(jnp.float32)
            taps.append(jnp.einsum('nijgc,nijgo->cgo', shifted, grads).reshape(group_width, channels))
    return jnp.stack(taps, axis=0)


def reference(activations, upstream, routes, gate_codes, weights):
    route_total = 2 * TILES
    slot_limit = CAP * N_EXPERT * N_DP

    def one_segment(segment_index):
        incoming = lax.dynamic_index_in_dim(upstream, (segment_index + 1) % SEGMENTS, 0, keepdims=False)
        inputs = lax.dynamic_index_in_dim(activations, segment_index, 0, keepdims=False)
        route_ids = lax.dynamic_index_in_dim(routes, segment_index, 0, keepdims=False)
        code_values = lax.dynamic_index_in_dim(gate_codes, segment_index, 0, keepdims=False).astype(jnp.float32)
        segment_weights = lax.dynamic_index_in_dim(weights, segment_index, 0, keepdims=False)
        gate_share = code_values / jnp.sum(code_values, axis=1, keepdims=True)
        scaled_grads = (gate_share[:, :, None, None] * incoming[:, None].astype(jnp.float32)).astype(jnp.bfloat16)
        flat_expert = route_ids.reshape(-1)
        matches = (flat_expert[:, None] == jnp.arange(EXPERTS, dtype=jnp.int32)[None, :]).astype(jnp.int32)
        earlier = jnp.cumsum(matches, axis=0) - matches
        slot_rank = jnp.sum(earlier * matches, axis=1).astype(jnp.int32)
        route_table = jnp.full((EXPERTS, slot_limit), route_total, jnp.int32)
        route_table = route_table.at[flat_expert, slot_rank].set(jnp.arange(route_total, dtype=jnp.int32))
        empty_row = jnp.zeros((1, TH * TW, C), jnp.bfloat16)
        grad_rows = jnp.concatenate([scaled_grads.reshape(route_total, TH * TW, C), empty_row], axis=0)
        input_rows = jnp.concatenate([jnp.repeat(inputs, 2, axis=0), empty_row], axis=0)

        def per_expert(expert_index):
            chosen = route_table[expert_index]
            grads_here = grad_rows[chosen]
            inputs_here = input_rows[chosen]
            kernel = lax.dynamic_index_in_dim(segment_weights, expert_index, 0, keepdims=False)
            answers = transpose_conv(grads_here, kernel).astype(jnp.bfloat16)
            return answers, weight_corr(inputs_here, grads_here, GW)

        answers, kernel_grads = lax.map(per_expert, jnp.arange(EXPERTS, dtype=jnp.int32))
        per_route = answers[flat_expert, slot_rank].astype(jnp.float32).reshape(TILES, 2, TH * TW, C)
        input_grad = (incoming.astype(jnp.float32) + per_route[:, 0] + per_route[:, 1]).astype(jnp.bfloat16)
        return input_grad, kernel_grads / TPD

    input_grad, weight_grad = lax.map(one_segment, jnp.arange(SEGMENTS, dtype=jnp.int32))
    return input_grad, weight_grad
```

```python
import functools
import math

import jax
import jax.numpy as jnp
from jax import lax
from jax.experimental import pallas as pl
from jax.experimental.pallas import tpu as pltpu
from jax.sharding import PartitionSpec as P

TH = 4
TW = 2
CELLS = TH * TW
CAP = 2
ROWS = CAP * CELLS
HALF = 256
TAPS = [(a, b) for a in (-1, 0, 1) for b in (-1, 0, 1)]
MESH = pl.DeviceIdType.MESH
NT = (((1,), (1,)), ((), ()))


def dot(a, b):
    return jnp.dot(a, b, preferred_element_type=jnp.float32)


def dot_nt(a, b):
    return lax.dot_general(a, b, NT, preferred_element_type=jnp.float32)


def iota(shape, axis):
    return lax.broadcasted_iota(jnp.int32, shape, axis)


def kernel(
    side, segments,
    routes_ref, codes_ref, x_ref, up_ref, w_ref,
    dx_ref, dw_ref,
    px, pd, an, xr, dr, ar, dy, choose, chooset, gates, dall, bd, xt, acc, dwm, dwo,
    send_sem, relay_sem, x_sem, d_sem, a_sem, dw_send, dw_sem,
):
    experts = side * side
    tiles = routes_ref.shape[1]
    channels = x_ref.shape[1]
    halves = channels // HALF
    gw = w_ref.shape[1]
    groups = HALF // gw
    block = side * ROWS

    seg = lax.axis_index("segment")
    me = lax.axis_index("expert")
    rep = lax.axis_index("dp")
    my_z, my_x = me // side, me % side

    def offsets(o):
        step_x = o % side
        return (o // side + step_x) % side, step_x

    def ahead(o):
        step_z, step_x = offsets(o)
        return ((my_z + step_z) % side) * side + (my_x + step_x) % side

    def behind(o):
        step_z, step_x = offsets(o)
        return ((my_z + side - step_z) % side) * side + (my_x + side - step_x) % side

    barrier = pltpu.get_barrier_semaphore()

    def greet(o, carry):
        pl.semaphore_signal(barrier, inc=1, device_id={"expert": ahead(o)}, device_id_type=MESH)
        return carry

    seg_before = (seg + segments - 1) % segments
    seg_after = (seg + 1) % segments
    pl.semaphore_signal(barrier, inc=1, device_id={"segment": seg_before}, device_id_type=MESH)
    pl.semaphore_signal(barrier, inc=1, device_id={"segment": seg_after}, device_id_type=MESH)
    pl.semaphore_signal(barrier, inc=1, device_id={"dp": 1 - rep}, device_id_type=MESH)
    lax.fori_loop(1, experts, greet, 0)

    first = routes_ref[0:1, :]
    second = routes_ref[1:2, :]
    codes = codes_ref[...].astype(jnp.float32)
    total = codes[0:1, :] + codes[1:2, :]
    gate_first = codes[0:1, :] / total
    gate_second = codes[1:2, :] / total
    earlier = (iota((tiles, tiles), 0) < iota((tiles, tiles), 1)).astype(jnp.bfloat16)
    spread = (iota((tiles, tiles * CELLS), 1) // CELLS == iota((tiles, tiles * CELLS), 0)).astype(
        jnp.bfloat16
    )
    same_cell = (
        iota((block, tiles * CELLS), 0) % CELLS == iota((block, tiles * CELLS), 1) % CELLS
    )

    def pack_x(k, carry):
        row = iota((block, tiles), 0)
        step_x = row // ROWS
        step_z = (step_x + k) % side
        expert = ((my_z + step_z) % side) * side + (my_x + step_x) % side
        slot = (row // CELLS) % CAP
        is_first = first == expert
        named = is_first | (second == expert)
        rank = dot(named.astype(jnp.float32).astype(jnp.bfloat16), earlier)
        taken = jnp.where(named & (rank == slot.astype(jnp.float32)), 1.0, 0.0)
        gate = jnp.sum(taken * jnp.where(is_first, gate_first, gate_second), axis=1, keepdims=True)
        rows = pl.ds(pl.multiple_of(k * block, block), block)
        gates[rows, :] = gate
        chosen = jnp.where(same_cell, dot(taken.astype(jnp.bfloat16), spread), 0.0).astype(
            jnp.bfloat16
        )
        choose[rows, :] = chosen
        packed = dot(chosen, x_ref[...]).astype(jnp.bfloat16)
        px[pl.ds(k * side, side)] = packed.reshape(side, ROWS, channels)
        return carry

    lax.fori_loop(0, side, pack_x, 0)

    pl.semaphore_wait(barrier, experts + 2)

    relay = pltpu.make_async_remote_copy(
        src_ref=up_ref, dst_ref=dy, send_sem=relay_sem.at[0], recv_sem=relay_sem.at[1],
        device_id={"segment": seg_before}, device_id_type=MESH,
    )
    relay.start()

    def send(source, target, o, kind, sem, device):
        pltpu.make_async_remote_copy(
            src_ref=source.at[o], dst_ref=target.at[o],
            send_sem=send_sem.at[kind], recv_sem=sem.at[o // side],
            device_id={"expert": device}, device_id_type=MESH,
        ).start()

    def keep(source, target, sem):
        pltpu.make_async_copy(source.at[0], target.at[0], sem.at[0]).start()

    def send_x(o, carry):
        send(px, xr, o, 0, x_sem, ahead(o))
        return carry

    keep(px, xr, x_sem)
    lax.fori_loop(1, experts, send_x, 0)

    same_group = iota((HALF, HALF), 0) // gw == iota((HALF, HALF), 1) // gw
    for half in range(halves):
        for tap in range(9):
            piece = w_ref[tap, :, half * HALF:(half + 1) * HALF]
            piled = jnp.concatenate([piece] * groups, axis=0)
            bd[half, :, tap * HALF:(tap + 1) * HALF] = jnp.where(
                same_group, piled, jnp.zeros_like(piled)
            )

    relay.wait_recv()

    def pack_d(k, carry):
        rows = pl.ds(pl.multiple_of(k * block, block), block)
        packed = (dot(choose[rows, :], dy[...]) * gates[rows, :]).astype(jnp.bfloat16)
        pd[pl.ds(k * side, side)] = packed.reshape(side, ROWS, channels)
        return carry

    lax.fori_loop(0, side, pack_d, 0)

    def send_d(o, carry):
        send(pd, dr, o, 1, d_sem, ahead(o))
        return carry

    keep(pd, dr, d_sem)
    lax.fori_loop(1, experts, send_d, 0)

    eye = (
        iota((tiles * CELLS, tiles * CELLS), 0) == iota((tiles * CELLS, tiles * CELLS), 1)
    ).astype(jnp.bfloat16)
    chooset[...] = dot_nt(eye, choose[...]).astype(jnp.bfloat16)

    def arrived(target, k, sem):
        part = target.at[pl.ds(k * side, side)]
        pltpu.make_async_copy(part, part, sem.at[k]).wait()

    tiles_here = side * CAP
    cell = iota((tiles_here, CELLS, HALF), 1)
    cell_i, cell_j = cell // TW, cell % TW

    def answer(k, carry):
        arrived(dr, k, d_sem)
        rows = pl.ds(pl.multiple_of(k * block, block), block)
        grads = dr[pl.ds(k * side, side)].reshape(block, channels)
        for half in range(halves):
            part = grads[:, half * HALF:(half + 1) * HALF]
            wide = part.astype(jnp.float32).reshape(tiles_here, CELLS, HALF)
            for tap, (a, b) in enumerate(TAPS):
                if a == 0 and b == 0:
                    moved = part
                else:
                    rolled = pltpu.roll(wide, (a * TW + b) % CELLS, 1)
                    valid = (
                        (cell_i - a >= 0) & (cell_i - a < TH) & (cell_j - b >= 0) & (cell_j - b < TW)
                    )
                    moved = jnp.where(valid, rolled, 0.0).reshape(block, HALF).astype(jnp.bfloat16)
                dall[half, rows, tap * HALF:(tap + 1) * HALF] = moved
            result = dot_nt(dall[half, rows, :], bd[half]).astype(jnp.bfloat16)
            an[pl.ds(k * side, side), :, half * HALF:(half + 1) * HALF] = result.reshape(
                side, ROWS, HALF
            )

        def send_a(j, inner):
            o = k * side + j

            @pl.when(o > 0)
            def _():
                send(an, ar, o, 2, a_sem, behind(o))

            @pl.when(o == 0)
            def _():
                keep(an, ar, a_sem)

            return inner

        lax.fori_loop(0, side, send_a, 0)
        return carry

    lax.fori_loop(0, side, answer, 0)

    all_x = xr.at[...]
    for k in range(side):
        arrived(xr, k, x_sem)
    eye_half = (iota((HALF, HALF), 0) == iota((HALF, HALF), 1)).astype(jnp.bfloat16)
    for half in range(halves):
        part = all_x[:, :, half * HALF:(half + 1) * HALF].reshape(experts * ROWS, HALF)
        xt[half] = dot_nt(eye_half, part).astype(jnp.bfloat16)

    lane_group = iota((gw, HALF), 1) // gw

    def swap(tap):
        return pltpu.make_async_remote_copy(
            src_ref=dwm.at[tap], dst_ref=dwo.at[tap],
            send_sem=dw_send.at[tap], recv_sem=dw_sem.at[tap],
            device_id={"dp": 1 - rep}, device_id_type=MESH,
        )

    for tap in range(9):
        for half in range(halves):
            full = dot(xt[half], dall[half, :, tap * HALF:(tap + 1) * HALF])
            picked = jnp.zeros((gw, HALF), jnp.float32)
            for g in range(groups):
                picked = jnp.where(lane_group == g, full[g * gw:(g + 1) * gw, :], picked)
            dwm[tap, :, half * HALF:(half + 1) * HALF] = picked
        swap(tap).start()

    acc[...] = dy[...].astype(jnp.float32)

    def combine(k, carry):
        arrived(ar, k, a_sem)
        rows = ar[pl.ds(k * side, side)].reshape(block, channels)
        cols = pl.ds(pl.multiple_of(k * block, block), block)
        acc[...] += dot(chooset[:, cols], rows)
        return carry

    lax.fori_loop(0, side, combine, 0)
    dx_ref[...] = acc[...].astype(jnp.bfloat16)

    for tap in range(9):
        swap(tap).wait_recv()
        dw_ref[tap] = (dwm[tap] + dwo[tap]) * (1.0 / tiles)

    relay.wait_send()
    for tap in range(9):
        swap(tap).wait_send()
    for kind, source in enumerate((px, pd, an)):
        sent = source.at[pl.ds(1, experts - 1)]
        pltpu.make_async_copy(sent, sent, send_sem.at[kind]).wait()


def body(side, segments, activations, upstream, routes, gate_codes, weights):
    _, tiles, cells, channels = activations.shape
    taps, gw = weights.shape[2], weights.shape[3]
    experts = side * side
    message = (experts, ROWS, channels)
    halves = channels // HALF
    vmem = pl.BlockSpec(memory_space=pltpu.VMEM)
    bf16, f32 = jnp.bfloat16, jnp.float32
    dma = pltpu.SemaphoreType.DMA
    input_grad, weight_grad = pl.pallas_call(
        functools.partial(kernel, side, segments),
        out_shape=(
            jax.ShapeDtypeStruct((tiles * cells, channels), bf16),
            jax.ShapeDtypeStruct((taps, gw, channels), f32),
        ),
        in_specs=[vmem] * 5,
        out_specs=(vmem, vmem),
        scratch_shapes=[pltpu.VMEM(message, bf16)] * 6
        + [
            pltpu.VMEM((tiles * cells, channels), bf16),
            pltpu.VMEM((experts * ROWS, tiles * cells), bf16),
            pltpu.VMEM((tiles * cells, experts * ROWS), bf16),
            pltpu.VMEM((experts * ROWS, 1), f32),
            pltpu.VMEM((halves, experts * ROWS, 9 * HALF), bf16),
            pltpu.VMEM((halves, HALF, 9 * HALF), bf16),
            pltpu.VMEM((halves, HALF, experts * ROWS), bf16),
            pltpu.VMEM((tiles * cells, channels), f32),
            pltpu.VMEM((taps, gw, channels), f32),
            pltpu.VMEM((taps, gw, channels), f32),
            dma((3,)), dma((2,)), dma((side,)), dma((side,)), dma((side,)), dma((9,)), dma((9,)),
        ],
        compiler_params=pltpu.CompilerParams(
            collective_id=0, has_side_effects=True, vmem_limit_bytes=56 * 1024 * 1024
        ),
    )(
        routes[0].T,
        gate_codes[0].T,
        activations.reshape(tiles * cells, channels),
        upstream.reshape(tiles * cells, channels),
        weights[0, 0],
    )
    return (
        input_grad.reshape(1, tiles, cells, channels),
        weight_grad.reshape(1, 1, taps, gw, channels),
    )


def solution(mesh):
    side = math.isqrt(mesh.shape["expert"])
    placed = (
        P("segment", ("expert", "dp"), None, None),
        P("segment", ("expert", "dp"), None, None),
        P("segment", ("expert", "dp"), None),
        P("segment", ("expert", "dp"), None),
        P("segment", "expert", None, None, None),
    )
    return jax.shard_map(
        functools.partial(body, side, mesh.shape["segment"]),
        mesh=mesh,
        in_specs=placed,
        out_specs=(
            P("segment", ("expert", "dp"), None, None),
            P("segment", "expert", None, None, None),
        ),
        check_vma=False,
    )
```

```python
import functools
import math

import jax
import jax.numpy as jnp
from jax import lax
from jax.experimental import pallas as pl
from jax.experimental.pallas import tpu as pltpu
from jax.sharding import PartitionSpec as P

TH = 4
TW = 2
CELLS = TH * TW
CAP = 2
ROWS = CAP * CELLS
HALF = 256
TAPS = [(a, b) for a in (-1, 0, 1) for b in (-1, 0, 1)]
MESH = pl.DeviceIdType.MESH
NT = (((1,), (1,)), ((), ()))


def dot(a, b):
    return jnp.dot(a, b, preferred_element_type=jnp.float32)


def dot_nt(a, b):
    return lax.dot_general(a, b, NT, preferred_element_type=jnp.float32)


def iota(shape, axis):
    return lax.broadcasted_iota(jnp.int32, shape, axis)


def kernel(
    side, segments,
    routes_ref, codes_ref, x_ref, up_ref, w_ref,
    dx_ref, dw_ref,
    px, pd, an, xr, dr, ar, dy, choose, chooset, gates, dall, bd, xt, acc, dwm, dwo,
    send_sem, relay_sem, x_sem, d_sem, a_sem, dw_send, dw_sem,
):
    experts = side * side
    tiles = routes_ref.shape[1]
    channels = x_ref.shape[1]
    halves = channels // HALF
    gw = w_ref.shape[1]
    groups = HALF // gw
    block = side * ROWS

    seg = lax.axis_index("segment")
    me = lax.axis_index("expert")
    rep = lax.axis_index("dp")
    my_z, my_x = me // side, me % side

    def offsets(o):
        step_x = o % side
        return (o // side + step_x) % side, step_x

    def ahead(o):
        step_z, step_x = offsets(o)
        return ((my_z + step_z) % side) * side + (my_x + step_x) % side

    def behind(o):
        step_z, step_x = offsets(o)
        return ((my_z + side - step_z) % side) * side + (my_x + side - step_x) % side

    barrier = pltpu.get_barrier_semaphore()

    def greet(o, carry):
        pl.semaphore_signal(barrier, inc=1, device_id={"expert": ahead(o)}, device_id_type=MESH)
        return carry

    seg_before = (seg + segments - 1) % segments
    seg_after = (seg + 1) % segments
    pl.semaphore_signal(barrier, inc=1, device_id={"segment": seg_before}, device_id_type=MESH)
    pl.semaphore_signal(barrier, inc=1, device_id={"segment": seg_after}, device_id_type=MESH)
    pl.semaphore_signal(barrier, inc=1, device_id={"dp": 1 - rep}, device_id_type=MESH)
    lax.fori_loop(1, experts, greet, 0)

    first = routes_ref[0:1, :]
    second = routes_ref[1:2, :]
    codes = codes_ref[...].astype(jnp.float32)
    total = codes[0:1, :] + codes[1:2, :]
    gate_first = codes[0:1, :] / total
    gate_second = codes[1:2, :] / total
    earlier = (iota((tiles, tiles), 0) < iota((tiles, tiles), 1)).astype(jnp.bfloat16)
    spread = (iota((tiles, tiles * CELLS), 1) // CELLS == iota((tiles, tiles * CELLS), 0)).astype(
        jnp.bfloat16
    )
    same_cell = (
        iota((block, tiles * CELLS), 0) % CELLS == iota((block, tiles * CELLS), 1) % CELLS
    )

    def pack_x(k):
        row = iota((block, tiles), 0)
        step_x = row // ROWS
        step_z = (step_x + k) % side
        expert = ((my_z + step_z) % side) * side + (my_x + step_x) % side
        slot = (row // CELLS) % CAP
        is_first = first == expert
        named = is_first | (second == expert)
        rank = dot(named.astype(jnp.float32).astype(jnp.bfloat16), earlier)
        taken = jnp.where(named & (rank == slot.astype(jnp.float32)), 1.0, 0.0)
        gate = jnp.sum(taken * jnp.where(is_first, gate_first, gate_second), axis=1, keepdims=True)
        rows = pl.ds(pl.multiple_of(k * block, block), block)
        gates[rows, :] = gate
        chosen = jnp.where(same_cell, dot(taken.astype(jnp.bfloat16), spread), 0.0).astype(
            jnp.bfloat16
        )
        choose[rows, :] = chosen
        packed = dot(chosen, x_ref[...]).astype(jnp.bfloat16)
        px[pl.ds(k * side, side)] = packed.reshape(side, ROWS, channels)

    pack_x(0)

    pl.semaphore_wait(barrier, experts + 2)

    relay = pltpu.make_async_remote_copy(
        src_ref=up_ref, dst_ref=dy, send_sem=relay_sem.at[0], recv_sem=relay_sem.at[1],
        device_id={"segment": seg_before}, device_id_type=MESH,
    )
    relay.start()

    def send(source, target, o, kind, sem, device):
        pltpu.make_async_remote_copy(
            src_ref=source.at[o], dst_ref=target.at[o],
            send_sem=send_sem.at[kind], recv_sem=sem.at[o // side],
            device_id={"expert": device}, device_id_type=MESH,
        ).start()

    def keep(source, target, sem):
        pltpu.make_async_copy(source.at[0], target.at[0], sem.at[0]).start()

    def send_x(o, carry):
        send(px, xr, o, 0, x_sem, ahead(o))
        return carry

    def dispatch_x(k, carry):
        pack_x(k)
        lax.fori_loop(k * side, (k + 1) * side, send_x, 0)
        return carry

    keep(px, xr, x_sem)
    lax.fori_loop(1, side, send_x, 0)
    lax.fori_loop(1, side, dispatch_x, 0)

    same_group = iota((HALF, HALF), 0) // gw == iota((HALF, HALF), 1) // gw
    for half in range(halves):
        for tap in range(9):
            piece = w_ref[tap, :, half * HALF:(half + 1) * HALF]
            piled = jnp.concatenate([piece] * groups, axis=0)
            bd[half, :, tap * HALF:(tap + 1) * HALF] = jnp.where(
                same_group, piled, jnp.zeros_like(piled)
            )

    relay.wait_recv()

    def pack_d(k):
        rows = pl.ds(pl.multiple_of(k * block, block), block)
        packed = (dot(choose[rows, :], dy[...]) * gates[rows, :]).astype(jnp.bfloat16)
        pd[pl.ds(k * side, side)] = packed.reshape(side, ROWS, channels)

    def send_d(o, carry):
        send(pd, dr, o, 1, d_sem, ahead(o))
        return carry

    def dispatch_d(k, carry):
        pack_d(k)
        lax.fori_loop(k * side, (k + 1) * side, send_d, 0)
        return carry

    pack_d(0)
    keep(pd, dr, d_sem)
    lax.fori_loop(1, side, send_d, 0)
    lax.fori_loop(1, side, dispatch_d, 0)

    eye = (
        iota((tiles * CELLS, tiles * CELLS), 0) == iota((tiles * CELLS, tiles * CELLS), 1)
    ).astype(jnp.bfloat16)
    chooset[...] = dot_nt(eye, choose[...]).astype(jnp.bfloat16)

    def arrived(target, k, sem):
        part = target.at[pl.ds(k * side, side)]
        pltpu.make_async_copy(part, part, sem.at[k]).wait()

    tiles_here = side * CAP
    cell = iota((tiles_here, CELLS, HALF), 1)
    cell_i, cell_j = cell // TW, cell % TW

    def answer(k, carry):
        arrived(dr, k, d_sem)
        rows = pl.ds(pl.multiple_of(k * block, block), block)
        grads = dr[pl.ds(k * side, side)].reshape(block, channels)
        for half in range(halves):
            part = grads[:, half * HALF:(half + 1) * HALF]
            wide = part.astype(jnp.float32).reshape(tiles_here, CELLS, HALF)
            for tap, (a, b) in enumerate(TAPS):
                if a == 0 and b == 0:
                    moved = part
                else:
                    rolled = pltpu.roll(wide, (a * TW + b) % CELLS, 1)
                    valid = (
                        (cell_i - a >= 0) & (cell_i - a < TH) & (cell_j - b >= 0) & (cell_j - b < TW)
                    )
                    moved = jnp.where(valid, rolled, 0.0).reshape(block, HALF).astype(jnp.bfloat16)
                dall[half, rows, tap * HALF:(tap + 1) * HALF] = moved
            result = dot_nt(dall[half, rows, :], bd[half]).astype(jnp.bfloat16)
            an[pl.ds(k * side, side), :, half * HALF:(half + 1) * HALF] = result.reshape(
                side, ROWS, HALF
            )

        def send_a(j, inner):
            o = k * side + j

            @pl.when(o > 0)
            def _():
                send(an, ar, o, 2, a_sem, behind(o))

            @pl.when(o == 0)
            def _():
                keep(an, ar, a_sem)

            return inner

        lax.fori_loop(0, side, send_a, 0)
        return carry

    lax.fori_loop(0, side, answer, 0)

    all_x = xr.at[...]
    for k in range(side):
        arrived(xr, k, x_sem)
    eye_half = (iota((HALF, HALF), 0) == iota((HALF, HALF), 1)).astype(jnp.bfloat16)
    for half in range(halves):
        part = all_x[:, :, half * HALF:(half + 1) * HALF].reshape(experts * ROWS, HALF)
        xt[half] = dot_nt(eye_half, part).astype(jnp.bfloat16)

    lane_group = iota((gw, HALF), 1) // gw

    def swap(tap):
        return pltpu.make_async_remote_copy(
            src_ref=dwm.at[tap], dst_ref=dwo.at[tap],
            send_sem=dw_send.at[tap], recv_sem=dw_sem.at[tap],
            device_id={"dp": 1 - rep}, device_id_type=MESH,
        )

    for tap in range(9):
        for half in range(halves):
            full = dot(xt[half], dall[half, :, tap * HALF:(tap + 1) * HALF])
            picked = jnp.zeros((gw, HALF), jnp.float32)
            for g in range(groups):
                picked = jnp.where(lane_group == g, full[g * gw:(g + 1) * gw, :], picked)
            dwm[tap, :, half * HALF:(half + 1) * HALF] = picked
        swap(tap).start()

    for tap in range(9):
        swap(tap).wait_recv()
        dw_ref[tap] = (dwm[tap] + dwo[tap]) * (1.0 / tiles)

    acc[...] = dy[...].astype(jnp.float32)

    def combine(k, carry):
        arrived(ar, k, a_sem)
        rows = ar[pl.ds(k * side, side)].reshape(block, channels)
        cols = pl.ds(pl.multiple_of(k * block, block), block)
        acc[...] += dot(chooset[:, cols], rows)
        return carry

    lax.fori_loop(0, side, combine, 0)
    dx_ref[...] = acc[...].astype(jnp.bfloat16)

    relay.wait_send()
    for tap in range(9):
        swap(tap).wait_send()
    for kind, source in enumerate((px, pd, an)):
        sent = source.at[pl.ds(1, experts - 1)]
        pltpu.make_async_copy(sent, sent, send_sem.at[kind]).wait()


def body(side, segments, activations, upstream, routes, gate_codes, weights):
    _, tiles, cells, channels = activations.shape
    taps, gw = weights.shape[2], weights.shape[3]
    experts = side * side
    message = (experts, ROWS, channels)
    halves = channels // HALF
    vmem = pl.BlockSpec(memory_space=pltpu.VMEM)
    bf16, f32 = jnp.bfloat16, jnp.float32
    dma = pltpu.SemaphoreType.DMA
    input_grad, weight_grad = pl.pallas_call(
        functools.partial(kernel, side, segments),
        out_shape=(
            jax.ShapeDtypeStruct((tiles * cells, channels), bf16),
            jax.ShapeDtypeStruct((taps, gw, channels), f32),
        ),
        in_specs=[vmem] * 5,
        out_specs=(vmem, vmem),
        scratch_shapes=[pltpu.VMEM(message, bf16)] * 6
        + [
            pltpu.VMEM((tiles * cells, channels), bf16),
            pltpu.VMEM((experts * ROWS, tiles * cells), bf16),
            pltpu.VMEM((tiles * cells, experts * ROWS), bf16),
            pltpu.VMEM((experts * ROWS, 1), f32),
            pltpu.VMEM((halves, experts * ROWS, 9 * HALF), bf16),
            pltpu.VMEM((halves, HALF, 9 * HALF), bf16),
            pltpu.VMEM((halves, HALF, experts * ROWS), bf16),
            pltpu.VMEM((tiles * cells, channels), f32),
            pltpu.VMEM((taps, gw, channels), f32),
            pltpu.VMEM((taps, gw, channels), f32),
            dma((3,)), dma((2,)), dma((side,)), dma((side,)), dma((side,)), dma((9,)), dma((9,)),
        ],
        compiler_params=pltpu.CompilerParams(
            collective_id=0, has_side_effects=True, vmem_limit_bytes=32 * 1024 * 1024
        ),
    )(
        routes[0].T,
        gate_codes[0].T,
        activations.reshape(tiles * cells, channels),
        upstream.reshape(tiles * cells, channels),
        weights[0, 0],
    )
    return (
        input_grad.reshape(1, tiles, cells, channels),
        weight_grad.reshape(1, 1, taps, gw, channels),
    )


def solution(mesh):
    side = math.isqrt(mesh.shape["expert"])
    placed = (
        P("segment", ("expert", "dp"), None, None),
        P("segment", ("expert", "dp"), None, None),
        P("segment", ("expert", "dp"), None),
        P("segment", ("expert", "dp"), None),
        P("segment", "expert", None, None, None),
    )
    return jax.shard_map(
        functools.partial(body, side, mesh.shape["segment"]),
        mesh=mesh,
        in_specs=placed,
        out_specs=(
            P("segment", ("expert", "dp"), None, None),
            P("segment", "expert", None, None, None),
        ),
        check_vma=False,
    )
```

```python
import functools
import math

import jax
import jax.numpy as jnp
from jax import lax
from jax.experimental import pallas as pl
from jax.experimental.pallas import tpu as pltpu
from jax.sharding import PartitionSpec as P

TH = 4
TW = 2
CELLS = TH * TW
CAP = 2
ROWS = CAP * CELLS
HALF = 256
TAPS = [(a, b) for a in (-1, 0, 1) for b in (-1, 0, 1)]
MESH = pl.DeviceIdType.MESH
NT = (((1,), (1,)), ((), ()))


def dot(a, b):
    return jnp.dot(a, b, preferred_element_type=jnp.float32)


def dot_nt(a, b):
    return lax.dot_general(a, b, NT, preferred_element_type=jnp.float32)


def iota(shape, axis):
    return lax.broadcasted_iota(jnp.int32, shape, axis)


def kernel(
    side, segments,
    routes_ref, codes_ref, x_ref, up_ref, w_ref,
    dx_ref, dw_ref,
    px, pd, an, xr, dr, ar, dy, choose, chooset, gates, dall, bd, xt, acc, dwm, dwo,
    send_sem, relay_sem, x_sem, d_sem, a_sem, dw_send, dw_sem, dw_out,
):
    experts = side * side
    tiles = routes_ref.shape[1]
    channels = x_ref.shape[1]
    halves = channels // HALF
    gw = w_ref.shape[1]
    groups = HALF // gw
    block = side * ROWS

    seg = lax.axis_index("segment")
    me = lax.axis_index("expert")
    rep = lax.axis_index("dp")
    my_z, my_x = me // side, me % side

    def offsets(o):
        step_x = o % side
        return (o // side + step_x) % side, step_x

    def ahead(o):
        step_z, step_x = offsets(o)
        return ((my_z + step_z) % side) * side + (my_x + step_x) % side

    def behind(o):
        step_z, step_x = offsets(o)
        return ((my_z + side - step_z) % side) * side + (my_x + side - step_x) % side

    barrier = pltpu.get_barrier_semaphore()

    def greet(o, carry):
        pl.semaphore_signal(barrier, inc=1, device_id={"expert": ahead(o)}, device_id_type=MESH)
        return carry

    seg_before = (seg + segments - 1) % segments
    seg_after = (seg + 1) % segments
    pl.semaphore_signal(barrier, inc=1, device_id={"segment": seg_before}, device_id_type=MESH)
    pl.semaphore_signal(barrier, inc=1, device_id={"segment": seg_after}, device_id_type=MESH)
    pl.semaphore_signal(barrier, inc=1, device_id={"dp": 1 - rep}, device_id_type=MESH)
    lax.fori_loop(1, experts, greet, 0)

    first = routes_ref[0:1, :]
    second = routes_ref[1:2, :]
    codes = codes_ref[...].astype(jnp.float32)
    total = codes[0:1, :] + codes[1:2, :]
    gate_first = codes[0:1, :] / total
    gate_second = codes[1:2, :] / total
    earlier = (iota((tiles, tiles), 0) < iota((tiles, tiles), 1)).astype(jnp.bfloat16)
    spread = (iota((tiles, tiles * CELLS), 1) // CELLS == iota((tiles, tiles * CELLS), 0)).astype(
        jnp.bfloat16
    )
    same_cell = (
        iota((block, tiles * CELLS), 0) % CELLS == iota((block, tiles * CELLS), 1) % CELLS
    )

    def pack_x(k, carry):
        row = iota((block, tiles), 0)
        step_x = row // ROWS
        step_z = (step_x + k) % side
        expert = ((my_z + step_z) % side) * side + (my_x + step_x) % side
        slot = (row // CELLS) % CAP
        is_first = first == expert
        named = is_first | (second == expert)
        rank = dot(named.astype(jnp.float32).astype(jnp.bfloat16), earlier)
        taken = jnp.where(named & (rank == slot.astype(jnp.float32)), 1.0, 0.0)
        gate = jnp.sum(taken * jnp.where(is_first, gate_first, gate_second), axis=1, keepdims=True)
        rows = pl.ds(pl.multiple_of(k * block, block), block)
        gates[rows, :] = gate
        chosen = jnp.where(same_cell, dot(taken.astype(jnp.bfloat16), spread), 0.0).astype(
            jnp.bfloat16
        )
        choose[rows, :] = chosen
        packed = dot(chosen, x_ref[...]).astype(jnp.bfloat16)
        px[pl.ds(k * side, side)] = packed.reshape(side, ROWS, channels)
        return carry

    lax.fori_loop(0, side, pack_x, 0)

    pl.semaphore_wait(barrier, experts + 2)

    relay = pltpu.make_async_remote_copy(
        src_ref=up_ref, dst_ref=dy, send_sem=relay_sem.at[0], recv_sem=relay_sem.at[1],
        device_id={"segment": seg_before}, device_id_type=MESH,
    )
    relay.start()

    def send(source, target, o, kind, sem, device):
        pltpu.make_async_remote_copy(
            src_ref=source.at[o], dst_ref=target.at[o],
            send_sem=send_sem.at[kind], recv_sem=sem.at[o // side],
            device_id={"expert": device}, device_id_type=MESH,
        ).start()

    def keep(source, target, sem):
        pltpu.make_async_copy(source.at[0], target.at[0], sem.at[0]).start()

    def send_x(o, carry):
        send(px, xr, o, 0, x_sem, ahead(o))
        return carry

    keep(px, xr, x_sem)
    lax.fori_loop(1, experts, send_x, 0)

    same_group = iota((HALF, HALF), 0) // gw == iota((HALF, HALF), 1) // gw
    for half in range(halves):
        for tap in range(9):
            piece = w_ref[tap, :, half * HALF:(half + 1) * HALF]
            piled = jnp.concatenate([piece] * groups, axis=0)
            bd[half, :, tap * HALF:(tap + 1) * HALF] = jnp.where(
                same_group, piled, jnp.zeros_like(piled)
            )

    relay.wait_recv()

    def pack_d(k, carry):
        rows = pl.ds(pl.multiple_of(k * block, block), block)
        packed = (dot(choose[rows, :], dy[...]) * gates[rows, :]).astype(jnp.bfloat16)
        pd[pl.ds(k * side, side)] = packed.reshape(side, ROWS, channels)
        return carry

    lax.fori_loop(0, side, pack_d, 0)

    def send_d(o, carry):
        send(pd, dr, o, 1, d_sem, ahead(o))
        return carry

    keep(pd, dr, d_sem)
    lax.fori_loop(1, experts, send_d, 0)

    eye = (
        iota((tiles * CELLS, tiles * CELLS), 0) == iota((tiles * CELLS, tiles * CELLS), 1)
    ).astype(jnp.bfloat16)
    chooset[...] = dot_nt(eye, choose[...]).astype(jnp.bfloat16)

    def arrived(target, k, sem):
        part = target.at[pl.ds(k * side, side)]
        pltpu.make_async_copy(part, part, sem.at[k]).wait()

    tiles_here = side * CAP
    cell = iota((tiles_here, CELLS, HALF), 1)
    cell_i, cell_j = cell // TW, cell % TW

    def answer(k, carry):
        arrived(dr, k, d_sem)
        rows = pl.ds(pl.multiple_of(k * block, block), block)
        grads = dr[pl.ds(k * side, side)].reshape(block, channels)
        for half in range(halves):
            part = grads[:, half * HALF:(half + 1) * HALF]
            wide = part.astype(jnp.float32).reshape(tiles_here, CELLS, HALF)
            for tap, (a, b) in enumerate(TAPS):
                if a == 0 and b == 0:
                    moved = part
                else:
                    rolled = pltpu.roll(wide, (a * TW + b) % CELLS, 1)
                    valid = (
                        (cell_i - a >= 0) & (cell_i - a < TH) & (cell_j - b >= 0) & (cell_j - b < TW)
                    )
                    moved = jnp.where(valid, rolled, 0.0).reshape(block, HALF).astype(jnp.bfloat16)
                dall[half, rows, tap * HALF:(tap + 1) * HALF] = moved
            result = dot_nt(dall[half, rows, :], bd[half]).astype(jnp.bfloat16)
            an[pl.ds(k * side, side), :, half * HALF:(half + 1) * HALF] = result.reshape(
                side, ROWS, HALF
            )

        def send_a(j, inner):
            o = k * side + j

            @pl.when(o > 0)
            def _():
                send(an, ar, o, 2, a_sem, behind(o))

            @pl.when(o == 0)
            def _():
                keep(an, ar, a_sem)

            return inner

        lax.fori_loop(0, side, send_a, 0)
        return carry

    lax.fori_loop(0, side, answer, 0)

    all_x = xr.at[...]
    for k in range(side):
        arrived(xr, k, x_sem)
    eye_half = (iota((HALF, HALF), 0) == iota((HALF, HALF), 1)).astype(jnp.bfloat16)
    for half in range(halves):
        part = all_x[:, :, half * HALF:(half + 1) * HALF].reshape(experts * ROWS, HALF)
        xt[half] = dot_nt(eye_half, part).astype(jnp.bfloat16)

    lane_group = iota((gw, HALF), 1) // gw

    def swap(tap):
        return pltpu.make_async_remote_copy(
            src_ref=dwm.at[tap], dst_ref=dwo.at[tap],
            send_sem=dw_send.at[tap], recv_sem=dw_sem.at[tap],
            device_id={"dp": 1 - rep}, device_id_type=MESH,
        )

    for tap in range(9):
        for half in range(halves):
            full = dot(xt[half], dall[half, :, tap * HALF:(tap + 1) * HALF])
            picked = jnp.zeros((gw, HALF), jnp.float32)
            for g in range(groups):
                picked = jnp.where(lane_group == g, full[g * gw:(g + 1) * gw, :], picked)
            dwm[tap, :, half * HALF:(half + 1) * HALF] = picked
        swap(tap).start()

    def stored(tap):
        return pltpu.make_async_copy(dwm.at[tap], dw_ref.at[tap], dw_out.at[tap])

    for tap in range(9):
        swap(tap).wait()
        dwm[tap] = (dwm[tap] + dwo[tap]) * (1.0 / tiles)
        stored(tap).start()

    acc[...] = dy[...].astype(jnp.float32)

    def combine(k, carry):
        arrived(ar, k, a_sem)
        rows = ar[pl.ds(k * side, side)].reshape(block, channels)
        cols = pl.ds(pl.multiple_of(k * block, block), block)
        acc[...] += dot(chooset[:, cols], rows)
        return carry

    lax.fori_loop(0, side, combine, 0)
    dx_ref[...] = acc[...].astype(jnp.bfloat16)

    relay.wait_send()
    for tap in range(9):
        stored(tap).wait()
    for kind, source in enumerate((px, pd, an)):
        sent = source.at[pl.ds(1, experts - 1)]
        pltpu.make_async_copy(sent, sent, send_sem.at[kind]).wait()


PIECES = 3


def hand_over_kernel(dx_in, dw_in, dx_out, dw_out, dx_held, dw_held, loads, stores):
    taps = dw_in.shape[0] // PIECES
    parts = [(dw_in.at[pl.ds(i * taps, taps)], dw_held.at[pl.ds(i * taps, taps)],
              dw_out.at[pl.ds(i * taps, taps)]) for i in range(PIECES)]
    parts.append((dx_in, dx_held, dx_out))
    loading = [pltpu.make_async_copy(a, b, loads.at[i]) for i, (a, b, _) in enumerate(parts)]
    storing = [pltpu.make_async_copy(b, c, stores.at[i]) for i, (_, b, c) in enumerate(parts)]
    for load in loading:
        load.start()
    for load, store in zip(loading, storing):
        load.wait()
        store.start()
    for store in storing:
        store.wait()


def hand_over(input_grad, weight_grad):
    hbm = pl.BlockSpec(memory_space=pltpu.HBM)
    arrays = (input_grad, weight_grad)
    return pl.pallas_call(
        hand_over_kernel,
        out_shape=tuple(jax.ShapeDtypeStruct(a.shape, a.dtype) for a in arrays),
        in_specs=[hbm, hbm],
        out_specs=(hbm, hbm),
        scratch_shapes=[pltpu.VMEM(a.shape, a.dtype) for a in arrays]
        + [pltpu.SemaphoreType.DMA((PIECES + 1,))] * 2,
        compiler_params=pltpu.CompilerParams(
            has_side_effects=True, vmem_limit_bytes=56 * 1024 * 1024
        ),
    )(*arrays)


def body(side, segments, activations, upstream, routes, gate_codes, weights):
    _, tiles, cells, channels = activations.shape
    taps, gw = weights.shape[2], weights.shape[3]
    experts = side * side
    message = (experts, ROWS, channels)
    halves = channels // HALF
    vmem = pl.BlockSpec(memory_space=pltpu.VMEM)
    bf16, f32 = jnp.bfloat16, jnp.float32
    dma = pltpu.SemaphoreType.DMA
    input_grad, weight_grad = pl.pallas_call(
        functools.partial(kernel, side, segments),
        out_shape=(
            jax.ShapeDtypeStruct((tiles * cells, channels), bf16),
            jax.ShapeDtypeStruct((taps, gw, channels), f32),
        ),
        in_specs=[vmem] * 5,
        out_specs=(vmem, pl.BlockSpec(memory_space=pltpu.HBM)),
        scratch_shapes=[pltpu.VMEM(message, bf16)] * 6
        + [
            pltpu.VMEM((tiles * cells, channels), bf16),
            pltpu.VMEM((experts * ROWS, tiles * cells), bf16),
            pltpu.VMEM((tiles * cells, experts * ROWS), bf16),
            pltpu.VMEM((experts * ROWS, 1), f32),
            pltpu.VMEM((halves, experts * ROWS, 9 * HALF), bf16),
            pltpu.VMEM((halves, HALF, 9 * HALF), bf16),
            pltpu.VMEM((halves, HALF, experts * ROWS), bf16),
            pltpu.VMEM((tiles * cells, channels), f32),
            pltpu.VMEM((taps, gw, channels), f32),
            pltpu.VMEM((taps, gw, channels), f32),
            dma((3,)), dma((2,)), dma((side,)), dma((side,)), dma((side,)), dma((9,)), dma((9,)), dma((9,)),
        ],
        compiler_params=pltpu.CompilerParams(
            collective_id=0, has_side_effects=True, vmem_limit_bytes=56 * 1024 * 1024
        ),
    )(
        routes[0].T,
        gate_codes[0].T,
        activations.reshape(tiles * cells, channels),
        upstream.reshape(tiles * cells, channels),
        weights[0, 0],
    )
    input_grad, weight_grad = hand_over(input_grad, weight_grad)
    return (
        input_grad.reshape(1, tiles, cells, channels),
        weight_grad.reshape(1, 1, taps, gw, channels),
    )


def solution(mesh):
    side = math.isqrt(mesh.shape["expert"])
    placed = (
        P("segment", ("expert", "dp"), None, None),
        P("segment", ("expert", "dp"), None, None),
        P("segment", ("expert", "dp"), None),
        P("segment", ("expert", "dp"), None),
        P("segment", "expert", None, None, None),
    )
    return jax.shard_map(
        functools.partial(body, side, mesh.shape["segment"]),
        mesh=mesh,
        in_specs=placed,
        out_specs=(
            P("segment", ("expert", "dp"), None, None),
            P("segment", "expert", None, None, None),
        ),
        check_vma=False,
    )
```
